512 devices in a mesh: rows: 128 (over x, z_lo, y), feat: 4 (over z_hi, core).
Axes of the slice: x: 4, y: 4, z: 16 (z_hi: 2, z_lo: 8; z = z_hi * 8 + z_lo), core: 2. Of those that a mesh axis runs over, the one named last changes fastest.
Arguments:
- features: bfloat16 [32768, 512], P('rows', 'feat'), may hold values from -6 to 6
- weight: bfloat16 [512, 512], P(None, 'feat'), may hold values from -0.25 to 0.25
- block_values: bfloat16 [256, 8, 128, 128], P('rows', 'feat'), may hold values from -0.25 to 0.25
- columns: int32 [256, 8], P('rows'), may hold values from 0 to 255, as said below
- counts: int32 [256], P('rows'), may hold values from 2 to 8, as said below
- cotangent: bfloat16 [32768, 512], P('rows', 'feat'), may hold values from -6 to 6
Outputs:
- hidden: bfloat16 [32768, 512], P('rows', 'feat')
- grad_features: bfloat16 [32768, 512], P('rows', 'feat')
- grad_weight: float32 [512, 512], P(None, 'feat')
The draws below stay inside these ranges and needn't reach their ends.
Inputs may be any that keep to these rules, and one draw needn't show every extreme that they name: `columns`: the 8 column blocks of a row block are distinct and lie on the devices within 4 indices of the row block's own index along rows, counted around the axis (the device of block c is c // 2). Slots 0 to counts[g] - 1 of row block g are live, the others are ignored; some row block has exactly 8 live slots.
All inputs are finite; a program needn't handle non-finite values.
Results may differ from the reference program's by a relative error of at most 0.0067.
Values may be sent and summed in bfloat16 or wider, within the bound.
No kernel may reach another device: no remote copies, remote signals or barrier semaphores. Data moves between devices by JAX's collectives and lax.ppermute only.
A program may use at most 64 MiB of HBM per device.

```python
import jax
import jax.numpy as jnp
from jax import lax

F = 512
O = 512
FB = 128
RB = 2
S = 8
REACH = 4
NRB = 256
NODES = 32768
N_ROWS = 128


def draw_columns(key, part):
    window_span = (2 * REACH + 1) * RB
    devices = NRB // RB
    scores = jax.random.randint(key, (NRB, window_span), 0, 1 << 20) * window_span + jnp.arange(window_span)
    chosen = lax.top_k(scores, S)[1]
    owner_dev = jnp.arange(NRB)[:, None] // RB
    target = (owner_dev + chosen // RB - REACH + devices) % devices
    return (target * RB + chosen % RB).astype(jnp.int32)


def draw_counts(key, part):
    devices = NRB // RB
    level_key = jax.random.fold_in(key, 11)
    count_key = jax.random.fold_in(key, 12)
    pick_key = jax.random.fold_in(key, 13)
    levels = jax.random.randint(level_key, (devices,), 0, 5)
    ceiling = 2 + (S - 2) * levels * levels // 16
    ceiling_rows = jnp.repeat(ceiling, RB)
    raw_draw = jax.random.randint(count_key, (NRB,), 0, 1 << 20)
    drawn = 2 + raw_draw % (ceiling_rows - 1)
    special = jax.random.randint(pick_key, (), 0, NRB)
    return jnp.where(jnp.arange(NRB) == special, S, drawn).astype(jnp.int32)


def shard_levels(key, extent, split, least, high):
    loudness = 1.0
    for axis_at, shards_of in split:
        draws = jax.random.uniform(jax.random.fold_in(jax.random.fold_in(key, 6), axis_at), (shards_of,), jnp.float32, least / len(split), high / len(split))
        loudness = loudness * jnp.repeat(jnp.exp(draws), extent[axis_at] // shards_of).reshape((-1,) + (1,) * (len(extent) - 1 - axis_at))
    return loudness


def gaussian(own_key, extent, scale, most, shards=(), held_as=jnp.bfloat16):
    level = shard_levels(own_key, extent, shards, -0.22, 0.18) if shards else 1.0
    result = jax.random.normal(own_key, extent, jnp.float32) * scale * level
    return jnp.minimum(jnp.maximum(result, -most), most).astype(held_as)


def setup_inputs(seed: int = 0) -> dict:
    splits = jax.random.split(jax.random.key(seed), 7)
    return {
        "features": gaussian(splits[0], (NODES, F), 1.0, 6.0, ((0, 128), (1, 4))),
        "weight": gaussian(splits[1], (F, O), F ** -0.5, 0.25, ((1, 4),)),
        "block_values": gaussian(splits[2], (NRB, S, FB, FB), (FB * S // 2) ** -0.5, 0.25, ((0, 128), (1, 4))),
        "columns": draw_columns(jax.random.fold_in(splits[6], 71), 0),
        "counts": draw_counts(jax.random.fold_in(splits[6], 71), 0),
        "cotangent": gaussian(splits[5], (NODES, O), 1.0, 6.0, ((0, 128), (1, 4))),
    }


def activation(values):
    return jax.nn.gelu(values, approximate=True)

def reference(features, weight, block_values, columns, counts, cotangent):
    row_total = counts.shape[0]
    block_size = block_values.shape[2]
    in_width = features.shape[1]
    feat_blocks = features.reshape(row_total, block_size, in_width)
    summed = jnp.zeros((row_total, block_size, in_width), jnp.float32)
    for slot_index in range(S):
        slot_live = (counts > slot_index).astype(jnp.float32)[:, None, None]
        picked = jnp.take(feat_blocks, columns[:, slot_index], axis=0).astype(jnp.float32)
        values_now = block_values[:, slot_index].astype(jnp.float32) * slot_live
        summed = summed + jnp.einsum('gij,gjf->gif', values_now, picked)
    aggregated = summed.reshape(NODES, in_width).astype(jnp.bfloat16)
    pre_act = jnp.dot(aggregated, weight, preferred_element_type=jnp.float32)
    hidden, act_grad = jax.vjp(activation, pre_act)
    grad_pre = act_grad(cotangent.astype(jnp.float32))[0].astype(jnp.bfloat16)
    grad_weight = lax.dot_general(aggregated, grad_pre, (((0,), (0,)), ((), ())), preferred_element_type=jnp.float32)
    grad_weight = grad_weight * float(NODES) ** (-0.5)
    grad_agg = lax.dot_general(grad_pre, weight, (((1,), (1,)), ((), ())), preferred_element_type=jnp.float32).astype(jnp.bfloat16)
    grad_blocks = grad_agg.reshape(row_total, block_size, in_width).astype(jnp.float32)
    span_count = 2 * REACH + 1
    center_mask = (jnp.arange(span_count) == REACH)[:, None, None, None]
    slot_ids = jnp.arange(S).astype(jnp.int32)

    def device_term(device, total):
        device = jnp.asarray(device).astype(jnp.int32)
        first = (device * RB).astype(jnp.int32)
        values_dev = lax.dynamic_slice_in_dim(block_values, first, RB, 0).astype(jnp.float32)
        cols_dev = lax.dynamic_slice_in_dim(columns, first, RB, 0).astype(jnp.int32)
        count_dev = lax.dynamic_slice_in_dim(counts, first, RB, 0).astype(jnp.int32)
        live = (slot_ids[None, :] < count_dev[:, None]).astype(jnp.float32)
        values_dev = values_dev * live[:, :, None, None]
        grads_dev = lax.dynamic_slice_in_dim(grad_blocks, first, RB, 0)
        products = jnp.einsum('gsij,gif->gsjf', values_dev, grads_dev)
        offsets = ((cols_dev // RB - device + REACH + N_ROWS) % N_ROWS).astype(jnp.int32)
        places = (offsets * RB + cols_dev % RB).astype(jnp.int32)
        window_sum = jnp.zeros((span_count * RB, block_size, in_width), jnp.float32)
        window_sum = window_sum.at[places.reshape(-1)].add(products.reshape(-1, block_size, in_width))
        window_sum = window_sum.reshape(span_count, RB, block_size, in_width)
        rounded = lax.optimization_barrier(window_sum.astype(jnp.bfloat16)).astype(jnp.float32)
        window_sum = jnp.where(center_mask, window_sum, rounded)
        owners = ((device + jnp.arange(span_count).astype(jnp.int32) - REACH + N_ROWS) % N_ROWS).astype(jnp.int32)
        targets = (owners[:, None] * RB + jnp.arange(RB).astype(jnp.int32)[None, :]).astype(jnp.int32)
        return total.at[targets.reshape(-1)].add(window_sum.reshape(-1, block_size, in_width))
    spread = lax.fori_loop(0, N_ROWS, device_term, jnp.zeros((row_total, block_size, in_width), jnp.float32))
    grad_features = spread.reshape(NODES, in_width).astype(jnp.bfloat16)
    return (hidden.astype(jnp.bfloat16), grad_features, grad_weight)
```

```python
import functools

import jax
import jax.numpy as jnp
from jax import lax
from jax.experimental import pallas as pl
from jax.experimental.pallas import tpu as pltpu
from jax.sharding import PartitionSpec as P

X, ZL, Y = 4, 8, 4
R = X * ZL * Y
FB = 128
RB = 2
REACH = 4
S = 8
GY = [[x * 32 + z * 4 + y for y in range(Y)] for x in range(X) for z in range(ZL)]
GZ = [[x * 32 + z * 4 + y for z in range(ZL)] for x in range(X) for y in range(Y)]
GXY = [[x * 32 + z * 4 + y for x in range(X) for y in range(Y)] for z in range(ZL)]
SWAP_A = [(r, (r + 4) % R if (r // 4) % 2 == 0 else (r - 4) % R) for r in range(R)]
SWAP_B = [(r, (r - 4) % R if (r // 4) % 2 == 0 else (r + 4) % R) for r in range(R)]
CROSS = [(f, f ^ 2) for f in range(4)]
SIBLING = [(f, f ^ 1) for f in range(4)]
FLIPS = (0, 2, 1, 3)
F32 = jnp.float32
BF16 = jnp.bfloat16


def window_place(col, r):
    y = r & 3
    off = ((col >> 1) - r + REACH + R) & (R - 1)
    t = y + off
    s = t & 3
    dq = (t >> 2) - 1
    piece = jnp.where(dq == 0, s * 2, jnp.where((dq == 1) & (s == y), 8, s * 2 + 1))
    return jnp.clip(piece * 2 + (col & 1), 0, 17)


def slot_of(p, j, f):
    return (f ^ FLIPS[p]) * 2 + j


def gather_kernel(ids, columns, counts, own, cross, pair, win, last, agg):
    r, f = ids[0], ids[1]
    for g in range(RB):
        total = jnp.zeros((FB, FB), F32)
        for p in range(4):
            for j in range(2):
                slot = slot_of(p, j, f)
                place = window_place(columns[g, slot], r)
                base = (g * 2 + j) * FB
                if p == 0:
                    tile = own[base : base + FB, :]
                elif p == 1:
                    tile = cross[base : base + FB, :]
                else:
                    start = (p - 2) * 1280 + base
                    tile = pair[start : start + FB, :]
                live = counts[g] > slot
                tile = jnp.where(live, tile, jnp.zeros_like(tile))
                block = win[place]
                total = total + jnp.dot(tile, block, preferred_element_type=F32)
        agg[g * FB : (g + 1) * FB, :] = total.astype(BF16)


def main_kernel(ids, columns, counts, own, cross, pair, agg, hidden, terms, mine, send, send_last, wnd, grad):
    r, f = ids[0], ids[1]
    y = r & 3
    k0 = 0.7978845608028654
    wide = jnp.concatenate([agg[k] for k in range(4)], axis=1)
    grad_agg = jnp.zeros((RB * FB, FB), F32)
    for p in range(4):
        ref, start = ((own, 0), (cross, 0), (pair, 0), (pair, 1280))[p]
        weight = ref[start + 768 : start + 1280, :]
        cot = ref[start + 512 : start + 768, :].astype(F32)
        v = jnp.dot(wide, weight, preferred_element_type=F32)
        v2 = v * v
        t = jnp.tanh(k0 * (v + 0.044715 * (v * v2)))
        half = 0.5 * (1.0 + t)
        if p == 0:
            hidden[...] = (v * half).astype(BF16)
        slope = half + 0.5 * v * (1.0 - t * t) * (k0 * (1.0 + 3 * 0.044715 * v2))
        grad_pre = (cot * slope).astype(BF16)
        if p == 0:
            terms[...] = lax.dot_general(
                wide, grad_pre, (((0,), (0,)), ((), ())), preferred_element_type=F32
            ).astype(BF16)
        rows = ref[pl.ds(pl.multiple_of(start + 768 + f * FB, FB), FB), :]
        grad_agg = grad_agg + lax.dot_general(
            grad_pre, rows, (((1,), (1,)), ((), ())), preferred_element_type=F32
        )
    grad[...] = grad_agg.astype(BF16)
    for b in range(18):
        wnd[b] = jnp.zeros((FB, FB), F32)
    for g in range(RB):
        part = grad[g * FB : (g + 1) * FB, :]
        for p in range(4):
            for j in range(2):
                slot = slot_of(p, j, f)
                place = window_place(columns[g, slot], r)
                ref, start = ((own, 0), (cross, 0), (pair, 0), (pair, 1280))[p]
                base = start + (g * 2 + j) * FB
                tile = ref[base : base + FB, :]
                live = counts[g] > slot
                tile = jnp.where(live, tile, jnp.zeros_like(tile))
                product = lax.dot_general(
                    tile, part, (((0,), (0,)), ((), ())), preferred_element_type=F32
                )
                wnd[place] = wnd[place] + product
    for b in range(16):
        send[b] = wnd[b].astype(BF16)
    for b in range(2):
        send_last[b] = wnd[16 + b]
        mine[b] = wnd[y * 4 + b]


def call(kernel, out_shape, scratch, *args):
    smem = pl.BlockSpec(memory_space=pltpu.SMEM)
    vmem = pl.BlockSpec(memory_space=pltpu.VMEM)
    return pl.pallas_call(
        kernel,
        out_shape=out_shape,
        in_specs=[smem] * 3 + [vmem] * (len(args) - 3),
        out_specs=jax.tree.map(lambda _: vmem, out_shape),
        scratch_shapes=scratch,
    )(*args)


def on_device(features, weight, block_values, columns, counts, cotangent):
    r = lax.axis_index("rows")
    f = lax.axis_index("feat")
    y = r % 4
    even = (r // 4) % 2 == 0
    ids = jnp.stack([r, f]).astype(jnp.int32)
    rows = features.shape[0]

    own = jnp.concatenate([block_values.reshape(4 * FB, FB), cotangent, weight], axis=0)
    cross = lax.ppermute(own, "feat", CROSS)
    from_b = lax.ppermute(features, "rows", SWAP_B)
    from_a = lax.ppermute(features, "rows", SWAP_A)
    nxt = jnp.where(even, from_a, from_b)
    prv = jnp.where(even, from_b, from_a)
    dest = jnp.arange(4)[:, None, None]
    extra = jnp.where(dest > y, nxt[None], prv[None])
    outgoing = jnp.stack([jnp.broadcast_to(features[None], (4, rows, FB)), extra], axis=1)
    arrived = lax.all_to_all(outgoing, "rows", 0, 0, axis_index_groups=GY, tiled=True)
    window = jnp.concatenate([arrived.reshape(16, FB, FB), nxt.reshape(2, FB, FB)], axis=0)
    pair = lax.ppermute(jnp.concatenate([own, cross], axis=0), "feat", SIBLING)

    agg = call(
        gather_kernel,
        jax.ShapeDtypeStruct((rows, FB), BF16),
        [],
        ids, columns, counts, own, cross, pair, window, nxt,
    )
    agg_full = lax.all_gather(agg, "feat", axis=0, tiled=False)
    hidden, terms, mine, send, send_last = call(
        main_kernel,
        (
            jax.ShapeDtypeStruct((rows, FB), BF16),
            jax.ShapeDtypeStruct((4 * FB, FB), BF16),
            jax.ShapeDtypeStruct((2, FB, FB), F32),
            jax.ShapeDtypeStruct((16, FB, FB), BF16),
            jax.ShapeDtypeStruct((2, FB, FB), F32),
        ),
        [pltpu.VMEM((18, FB, FB), F32), pltpu.VMEM((rows, FB), BF16)],
        ids, columns, counts, own, cross, pair, agg_full,
    )

    got = lax.all_to_all(
        send.reshape(4, 2, rows, FB), "rows", 0, 0, axis_index_groups=GY, tiled=True
    ).astype(F32)
    source = jnp.arange(4)[:, None, None]
    here = mine.reshape(rows, FB) + jnp.where(source == y, 0.0, got[:, 0]).sum(0)
    to_prv = jnp.where(source <= y, got[:, 1], 0.0).sum(0)
    to_nxt = jnp.where(source > y, got[:, 1], 0.0).sum(0) + send_last.reshape(rows, FB)
    to_prv, to_nxt = to_prv.astype(BF16), to_nxt.astype(BF16)
    back_b = lax.ppermute(jnp.where(even, to_prv, to_nxt), "rows", SWAP_B)
    back_a = lax.ppermute(jnp.where(even, to_nxt, to_prv), "rows", SWAP_A)
    grad_features = (here + back_a.astype(F32) + back_b.astype(F32)).astype(BF16)

    parts = lax.all_to_all(terms.reshape(16, 32, FB), "rows", 0, 0, axis_index_groups=GXY, tiled=True)
    part = parts.astype(F32).sum(0)
    layers = lax.all_to_all(
        jnp.broadcast_to(part[None], (8, 32, FB)), "rows", 0, 0, axis_index_groups=GZ, tiled=True
    )
    total = (layers.sum(0) * float(rows * R) ** (-0.5)).astype(BF16)
    grad_weight = lax.all_to_all(
        jnp.broadcast_to(total[None], (16, 32, FB)), "rows", 0, 0, axis_index_groups=GXY, tiled=True
    )
    return hidden, grad_features, grad_weight.reshape(4 * FB, FB).astype(F32)


def solution(mesh):
    in_specs = (
        P("rows", "feat"),
        P(None, "feat"),
        P("rows", "feat", None, None),
        P("rows", None),
        P("rows"),
        P("rows", "feat"),
    )
    out_specs = (P("rows", "feat"), P("rows", "feat"), P(None, "feat"))
    return jax.shard_map(
        on_device, mesh=mesh, in_specs=in_specs, out_specs=out_specs, check_vma=False
    )
```

```python
import jax
import jax.numpy as jnp
from jax import lax
from jax.experimental import pallas as pl
from jax.experimental.pallas import tpu as pltpu
from jax.sharding import PartitionSpec as P


X, ZL, Y = 4, 8, 4
R = X * ZL * Y
FB = 128
RB = 2
REACH = 4
STEP_Y = [[(r, r // 4 * 4 + (r + k) % 4) for r in range(R)] for k in range(4)]
SWAP_A = [(r, (r + 4) % R if (r // 4) % 2 == 0 else (r - 4) % R) for r in range(R)]
SWAP_B = [(r, (r - 4) % R if (r // 4) % 2 == 0 else (r + 4) % R) for r in range(R)]
CROSS = [(f, f ^ 2) for f in range(4)]
SIBLING = [(f, f ^ 1) for f in range(4)]
FLIPS = (0, 2, 1, 3)
F32 = jnp.float32
BF16 = jnp.bfloat16


def window_place(col, r, sign):
    y = r & 3
    off = ((col >> 1) - r + REACH + R) & (R - 1)
    t = y + off
    s = t & 3
    dq = (t >> 2) - 1
    k = (sign * (s - y)) & 3
    piece = jnp.where(dq == 0, k * 2, jnp.where((dq == 1) & (k == 0), 8, k * 2 + 1))
    return jnp.clip(piece * 2 + (col & 1), 0, 17)


def slot_of(p, j, f):
    return (f ^ FLIPS[p]) * 2 + j


def panel_tile(refs, p, g, j):
    own, cross, pair = refs
    ref, start = ((own, 0), (cross, 0), (pair, 0), (pair, 4 * FB))[p]
    base = start + (g * 2 + j) * FB
    return ref[base : base + FB, :]


def gather_kernel(ids, columns, counts, own, cross, pair, near, before, win1, win2, win3, after, agg, win):
    r, f = ids[0], ids[1]
    for start, ref in ((0, near), (2, before), (4, win1), (8, win2), (12, win3), (16, after)):
        win[start : start + ref.shape[0]] = ref[...]
    for g in range(RB):
        total = jnp.zeros((FB, FB), F32)
        for p in range(4):
            for j in range(2):
                slot = slot_of(p, j, f)
                place = window_place(columns[g, slot], r, -1)
                tile = panel_tile((own, cross, pair), p, g, j)
                tile = jnp.where(counts[g] > slot, tile, jnp.zeros_like(tile))
                block = win[place]
                total = total + jnp.dot(tile, block, preferred_element_type=F32)
        agg[g * FB : (g + 1) * FB, :] = total.astype(BF16)


def layer_kernel(ids, own, cross, pair, agg, hidden, terms, grad):
    f = ids[1]
    k0 = 0.7978845608028654
    wide = jnp.concatenate([agg[k] for k in range(4)], axis=1)
    grad_agg = jnp.zeros((RB * FB, FB), F32)
    for p in range(4):
        ref, start = ((own, 0), (cross, 0), (pair, 0), (pair, 6 * FB))[p]
        weight = ref[start + 2 * FB : start + 6 * FB, :]
        cot = ref[start : start + 2 * FB, :].astype(F32)
        v = jnp.dot(wide, weight, preferred_element_type=F32)
        v2 = v * v
        t = jnp.tanh(k0 * (v + 0.044715 * (v * v2)))
        half = 0.5 * (1.0 + t)
        if p == 0:
            hidden[...] = (v * half).astype(BF16)
        slope = half + 0.5 * v * (1.0 - t * t) * (k0 * (1.0 + 3 * 0.044715 * v2))
        grad_pre = (cot * slope).astype(BF16)
        if p == 0:
            terms[...] = lax.dot_general(
                wide, grad_pre, (((0,), (0,)), ((), ())), preferred_element_type=F32
            ).astype(BF16)
        rows = ref[pl.ds(pl.multiple_of(start + 2 * FB + f * FB, FB), FB), :]
        grad_agg = grad_agg + lax.dot_general(
            grad_pre, rows, (((1,), (1,)), ((), ())), preferred_element_type=F32
        )
    grad[...] = grad_agg.astype(BF16)


def spread_kernel(ids, columns, counts, own, cross, pair, grad, mine, send1, send2, send3, wnd):
    r, f = ids[0], ids[1]
    for b in range(18):
        wnd[b] = jnp.zeros((FB, FB), F32)
    for g in range(RB):
        part = grad[g * FB : (g + 1) * FB, :]
        for p in range(4):
            for j in range(2):
                slot = slot_of(p, j, f)
                place = window_place(columns[g, slot], r, 1)
                tile = panel_tile((own, cross, pair), p, g, j)
                tile = jnp.where(counts[g] > slot, tile, jnp.zeros_like(tile))
                product = lax.dot_general(
                    tile, part, (((0,), (0,)), ((), ())), preferred_element_type=F32
                )
                wnd[place] = wnd[place] + product
    for k, ref in ((1, send1), (2, send2), (3, send3)):
        for b in range(4):
            ref[b] = wnd[k * 4 + b].astype(BF16)
    for b in range(4):
        mine[b] = wnd[b]
    for b in range(2):
        mine[4 + b] = wnd[16 + b]


def call(kernel, out_shape, scratch, scalars, *args):
    smem = pl.BlockSpec(memory_space=pltpu.SMEM)
    vmem = pl.BlockSpec(memory_space=pltpu.VMEM)
    return pl.pallas_call(
        kernel,
        out_shape=out_shape,
        in_specs=[smem] * len(scalars) + [vmem] * len(args),
        out_specs=jax.tree.map(lambda _: vmem, out_shape),
        scratch_shapes=scratch,
    )(*scalars, *args)


def blocks(value):
    return value.reshape(-1, FB, FB)


def on_device(features, weight, block_values, columns, counts, cotangent):
    r = lax.axis_index("rows")
    f = lax.axis_index("feat")
    y = r & 3
    even = ((r >> 2) & 1) == 0
    ids = jnp.stack([r, f]).astype(jnp.int32)
    rows = features.shape[0]

    from_b = lax.ppermute(features, "rows", SWAP_B)
    from_a = lax.ppermute(features, "rows", SWAP_A)
    own_p = block_values.reshape(4 * FB, FB)
    cross_p = lax.ppermute(own_p, "feat", CROSS)
    own_w = jnp.concatenate([cotangent, weight], axis=0)
    cross_w = lax.ppermute(own_w, "feat", CROSS)
    nxt = jnp.where(even, from_a, from_b)
    prv = jnp.where(even, from_b, from_a)
    arrived = []
    for k in range(1, 4):
        extra = jnp.where(y < 4 - k, nxt, prv)
        arrived.append(lax.ppermute(jnp.stack([features, extra]), "rows", STEP_Y[k]))
    cross_p, *arrived = lax.optimization_barrier((cross_p, *arrived))
    pair_p = lax.ppermute(jnp.concatenate([own_p, cross_p], axis=0), "feat", SIBLING)
    agg = call(
        gather_kernel,
        jax.ShapeDtypeStruct((rows, FB), BF16),
        [pltpu.VMEM((18, FB, FB), BF16)],
        (ids, columns, counts),
        own_p, cross_p, pair_p, blocks(features), blocks(prv), *map(blocks, arrived), blocks(nxt),
    )
    cross_w, agg = lax.optimization_barrier((cross_w, agg))
    pair_w = lax.ppermute(jnp.concatenate([own_w, cross_w], axis=0), "feat", SIBLING)
    agg_full = lax.all_gather(agg, "feat", axis=0, tiled=False)
    hidden, terms, grad = call(
        layer_kernel,
        (
            jax.ShapeDtypeStruct((rows, FB), BF16),
            jax.ShapeDtypeStruct((4 * FB, FB), BF16),
            jax.ShapeDtypeStruct((rows, FB), BF16),
        ),
        [],
        (ids,),
        own_w, cross_w, pair_w, agg_full,
    )
    parts = lax.all_to_all(terms.reshape(R, 4, FB), "rows", 0, 0, tiled=True)
    mine, *sends = call(
        spread_kernel,
        (
            jax.ShapeDtypeStruct((6, FB, FB), F32),
            jax.ShapeDtypeStruct((4, FB, FB), BF16),
            jax.ShapeDtypeStruct((4, FB, FB), BF16),
            jax.ShapeDtypeStruct((4, FB, FB), BF16),
        ),
        [pltpu.VMEM((18, FB, FB), F32)],
        (ids, columns, counts),
        own_p, cross_p, pair_p, grad,
    )
    got = []
    for k in range(1, 4):
        got.append(lax.ppermute(sends[k - 1].reshape(2, rows, FB), "rows", STEP_Y[k]).astype(F32))
    here, to_prv, to_nxt = mine.reshape(3, rows, FB)
    for k in range(1, 4):
        here = here + got[k - 1][0]
        to_prv = to_prv + jnp.where(y >= k, got[k - 1][1], 0.0)
        to_nxt = to_nxt + jnp.where(y < k, got[k - 1][1], 0.0)
    to_prv, to_nxt = to_prv.astype(BF16), to_nxt.astype(BF16)
    back_b = lax.ppermute(jnp.where(even, to_prv, to_nxt), "rows", SWAP_B)
    back_a = lax.ppermute(jnp.where(even, to_nxt, to_prv), "rows", SWAP_A)
    grad_features = (here + back_a.astype(F32) + back_b.astype(F32)).astype(BF16)

    total = (parts.astype(F32).sum(0) * float(rows * R) ** (-0.5)).astype(BF16)
    grad_weight = lax.all_to_all(
        jnp.broadcast_to(total[None], (R, 4, FB)), "rows", 0, 0, tiled=True
    )
    return hidden, grad_features, grad_weight.reshape(4 * FB, FB).astype(F32)


def solution(mesh):
    in_specs = (
        P("rows", "feat"),
        P(None, "feat"),
        P("rows", "feat", None, None),
        P("rows", None),
        P("rows"),
        P("rows", "feat"),
    )
    out_specs = (P("rows", "feat"), P("rows", "feat"), P(None, "feat"))
    return jax.shard_map(
        on_device, mesh=mesh, in_specs=in_specs, out_specs=out_specs, check_vma=False
    )
```

```python
import jax
import jax.numpy as jnp
from jax import lax
from jax.experimental import pallas as pl
from jax.experimental.pallas import tpu as pltpu
from jax.sharding import PartitionSpec as P


X, ZL, Y = 4, 8, 4
R = X * ZL * Y
FB = 128
RB = 2
REACH = 4
STEP_Y = [[(r, r // 4 * 4 + (r + k) % 4) for r in range(R)] for k in range(4)]
GZ = [[x * 32 + z * 4 + y for z in range(ZL)] for x in range(X) for y in range(Y)]
GXY = [[x * 32 + z * 4 + y for x in range(X) for y in range(Y)] for z in range(ZL)]
SWAP_A = [(r, (r + 4) % R if (r // 4) % 2 == 0 else (r - 4) % R) for r in range(R)]
SWAP_B = [(r, (r - 4) % R if (r // 4) % 2 == 0 else (r + 4) % R) for r in range(R)]
CROSS = [(f, f ^ 2) for f in range(4)]
SIBLING = [(f, f ^ 1) for f in range(4)]
FLIPS = (0, 2, 1, 3)
F32 = jnp.float32
BF16 = jnp.bfloat16


def window_place(col, r, sign):
    y = r & 3
    off = ((col >> 1) - r + REACH + R) & (R - 1)
    t = y + off
    s = t & 3
    dq = (t >> 2) - 1
    k = (sign * (s - y)) & 3
    piece = jnp.where(dq == 0, k * 2, jnp.where((dq == 1) & (k == 0), 8, k * 2 + 1))
    return jnp.clip(piece * 2 + (col & 1), 0, 17)


def slot_of(p, j, f):
    return (f ^ FLIPS[p]) * 2 + j


def panel_tile(refs, p, g, j):
    own, cross, pair = refs
    ref, start = ((own, 0), (cross, 0), (pair, 0), (pair, 4 * FB))[p]
    base = start + (g * 2 + j) * FB
    return ref[base : base + FB, :]


def gather_kernel(ids, columns, counts, own, cross, pair, near, before, win1, win2, win3, after, agg, win):
    r, f = ids[0], ids[1]
    for start, ref in ((0, near), (2, before), (4, win1), (8, win2), (12, win3), (16, after)):
        win[start : start + ref.shape[0]] = ref[...]
    for g in range(RB):
        total = jnp.zeros((FB, FB), F32)
        for p in range(4):
            for j in range(2):
                slot = slot_of(p, j, f)
                place = window_place(columns[g, slot], r, -1)
                tile = panel_tile((own, cross, pair), p, g, j)
                tile = jnp.where(counts[g] > slot, tile, jnp.zeros_like(tile))
                block = win[place]
                total = total + jnp.dot(tile, block, preferred_element_type=F32)
        agg[g * FB : (g + 1) * FB, :] = total.astype(BF16)


def layer_kernel(ids, own, cross, pair, agg, hidden, terms, grad):
    f = ids[1]
    k0 = 0.7978845608028654
    wide = jnp.concatenate([agg[k] for k in range(4)], axis=1)
    grad_agg = jnp.zeros((RB * FB, FB), F32)
    for p in range(4):
        ref, start = ((own, 0), (cross, 0), (pair, 0), (pair, 6 * FB))[p]
        weight = ref[start + 2 * FB : start + 6 * FB, :]
        cot = ref[start : start + 2 * FB, :].astype(F32)
        v = jnp.dot(wide, weight, preferred_element_type=F32)
        v2 = v * v
        t = jnp.tanh(k0 * (v + 0.044715 * (v * v2)))
        half = 0.5 * (1.0 + t)
        if p == 0:
            hidden[...] = (v * half).astype(BF16)
        slope = half + 0.5 * v * (1.0 - t * t) * (k0 * (1.0 + 3 * 0.044715 * v2))
        grad_pre = (cot * slope).astype(BF16)
        if p == 0:
            terms[...] = lax.dot_general(
                wide, grad_pre, (((0,), (0,)), ((), ())), preferred_element_type=F32
            ).astype(BF16)
        rows = ref[pl.ds(pl.multiple_of(start + 2 * FB + f * FB, FB), FB), :]
        grad_agg = grad_agg + lax.dot_general(
            grad_pre, rows, (((1,), (1,)), ((), ())), preferred_element_type=F32
        )
    grad[...] = grad_agg.astype(BF16)


def spread_kernel(ids, columns, counts, own, cross, pair, grad, mine, send1, send2, send3, wnd):
    r, f = ids[0], ids[1]
    for b in range(18):
        wnd[b] = jnp.zeros((FB, FB), F32)
    for g in range(RB):
        part = grad[g * FB : (g + 1) * FB, :]
        for p in range(4):
            for j in range(2):
                slot = slot_of(p, j, f)
                place = window_place(columns[g, slot], r, 1)
                tile = panel_tile((own, cross, pair), p, g, j)
                tile = jnp.where(counts[g] > slot, tile, jnp.zeros_like(tile))
                product = lax.dot_general(
                    tile, part, (((0,), (0,)), ((), ())), preferred_element_type=F32
                )
                wnd[place] = wnd[place] + product
    for k, ref in ((1, send1), (2, send2), (3, send3)):
        for b in range(4):
            ref[b] = wnd[k * 4 + b].astype(BF16)
    for b in range(4):
        mine[b] = wnd[b]
    for b in range(2):
        mine[4 + b] = wnd[16 + b]


def call(kernel, out_shape, scratch, scalars, *args):
    smem = pl.BlockSpec(memory_space=pltpu.SMEM)
    vmem = pl.BlockSpec(memory_space=pltpu.VMEM)
    return pl.pallas_call(
        kernel,
        out_shape=out_shape,
        in_specs=[smem] * len(scalars) + [vmem] * len(args),
        out_specs=jax.tree.map(lambda _: vmem, out_shape),
        scratch_shapes=scratch,
    )(*scalars, *(pltpu.with_memory_space_constraint(value, pltpu.VMEM) for value in args))


def blocks(value):
    return value.reshape(-1, FB, FB)


def on_device(features, weight, block_values, columns, counts, cotangent):
    r = lax.axis_index("rows")
    f = lax.axis_index("feat")
    y = r & 3
    even = ((r >> 2) & 1) == 0
    ids = jnp.stack([r, f]).astype(jnp.int32)
    rows = features.shape[0]

    from_b = lax.ppermute(features, "rows", SWAP_B)
    from_a = lax.ppermute(features, "rows", SWAP_A)
    own_p = block_values.reshape(4 * FB, FB)
    cross_p = lax.ppermute(own_p, "feat", CROSS)
    own_w = jnp.concatenate([cotangent, weight], axis=0)
    cross_w = lax.ppermute(own_w, "feat", CROSS)
    nxt = jnp.where(even, from_a, from_b)
    prv = jnp.where(even, from_b, from_a)
    arrived = []
    for k in range(1, 4):
        extra = jnp.where(y < 4 - k, nxt, prv)
        arrived.append(lax.ppermute(jnp.stack([features, extra]), "rows", STEP_Y[k]))
    cross_p, *arrived = lax.optimization_barrier((cross_p, *arrived))
    pair_p = lax.ppermute(jnp.concatenate([own_p, cross_p], axis=0), "feat", SIBLING)
    agg = call(
        gather_kernel,
        jax.ShapeDtypeStruct((rows, FB), BF16),
        [pltpu.VMEM((18, FB, FB), BF16)],
        (ids, columns, counts),
        own_p, cross_p, pair_p, blocks(features), blocks(prv), *map(blocks, arrived), blocks(nxt),
    )
    cross_w, agg = lax.optimization_barrier((cross_w, agg))
    pair_w = lax.ppermute(jnp.concatenate([own_w, cross_w], axis=0), "feat", SIBLING)
    agg_full = lax.all_gather(agg, "feat", axis=0, tiled=False)
    hidden, terms, grad = call(
        layer_kernel,
        (
            jax.ShapeDtypeStruct((rows, FB), BF16),
            jax.ShapeDtypeStruct((4 * FB, FB), BF16),
            jax.ShapeDtypeStruct((rows, FB), BF16),
        ),
        [],
        (ids,),
        own_w, cross_w, pair_w, agg_full,
    )
    parts = lax.all_to_all(
        terms.reshape(16, 32, FB), "rows", 0, 0, axis_index_groups=GXY, tiled=True
    )
    mine, *sends = call(
        spread_kernel,
        (
            jax.ShapeDtypeStruct((6, FB, FB), F32),
            jax.ShapeDtypeStruct((4, FB, FB), BF16),
            jax.ShapeDtypeStruct((4, FB, FB), BF16),
            jax.ShapeDtypeStruct((4, FB, FB), BF16),
        ),
        [pltpu.VMEM((18, FB, FB), F32)],
        (ids, columns, counts),
        own_p, cross_p, pair_p, grad,
    )
    got = []
    for k in range(1, 4):
        got.append(lax.ppermute(sends[k - 1].reshape(2, rows, FB), "rows", STEP_Y[k]).astype(F32))
    part = parts.astype(F32).sum(0)
    layers = lax.all_to_all(jnp.broadcast_to(part[None], (8, 32, FB)), "rows", 0, 0, axis_index_groups=GZ, tiled=True)
    here, to_prv, to_nxt = mine.reshape(3, rows, FB)
    for k in range(1, 4):
        here = here + got[k - 1][0]
        to_prv = to_prv + jnp.where(y >= k, got[k - 1][1], 0.0)
        to_nxt = to_nxt + jnp.where(y < k, got[k - 1][1], 0.0)
    to_prv, to_nxt = to_prv.astype(BF16), to_nxt.astype(BF16)
    back_b = lax.ppermute(jnp.where(even, to_prv, to_nxt), "rows", SWAP_B)
    back_a = lax.ppermute(jnp.where(even, to_nxt, to_prv), "rows", SWAP_A)
    grad_features = (here + back_a.astype(F32) + back_b.astype(F32)).astype(BF16)

    total = (layers.sum(0) * float(rows * R) ** (-0.5)).astype(BF16)
    grad_weight = lax.all_to_all(
        jnp.broadcast_to(total[None], (16, 32, FB)), "rows", 0, 0, axis_index_groups=GXY, tiled=True
    )
    return hidden, grad_features, grad_weight.reshape(4 * FB, FB).astype(F32)


def solution(mesh):
    in_specs = (
        P("rows", "feat"),
        P(None, "feat"),
        P("rows", "feat", None, None),
        P("rows", None),
        P("rows"),
        P("rows", "feat"),
    )
    out_specs = (P("rows", "feat"), P("rows", "feat"), P(None, "feat"))
    return jax.shard_map(on_device, mesh=mesh, in_specs=in_specs, out_specs=out_specs, check_vma=False)
```
